32 devices in a mesh: ctx: 16 (over z, x, core), fsdp: 2 (over y).
Axes of the slice: x: 2, y: 2, z: 4, core: 2. Of those that a mesh axis runs over, the one named last changes fastest.
Arguments:
- tokens: float32 [4, 6144, 768], P('fsdp', 'ctx'), may hold values from -6 to 6
- w_query: float32 [768, 768], P('fsdp'), may hold values from -0.21875 to 0.21875
- w_key: float32 [768, 768], P('fsdp'), may hold values from -0.21875 to 0.21875
- w_value: float32 [768, 768], P('fsdp'), may hold values from -0.21875 to 0.21875
- w_mixer: float32 [768, 768], P('fsdp'), may hold values from -3.5 to 3.5
- w_inner: float32 [768, 3072], P('fsdp'), may hold values from -0.21875 to 0.21875
- b_inner: float32 [3072], P('fsdp'), may hold values from -3 to 3
- w_outer: float32 [3072, 768], P('fsdp'), may hold values from -0.109375 to 0.109375
- b_outer: float32 [768], P('fsdp'), may hold values from -3 to 3
- gain_one: float32 [768], P('fsdp'), may hold values from 0.5 to 1.5
- shift_one: float32 [768], P('fsdp'), may hold values from -3 to 3
- gain_two: float32 [768], P('fsdp'), may hold values from 0.5 to 1.5
- shift_two: float32 [768], P('fsdp'), may hold values from -3 to 3
- seq_lengths: int32 [4], replicated, may hold values from 1 to 6144, 12288 in all
- rotation: int32 [4], replicated, may hold values from 0 to 15
- cotangent: float32 [4, 6144, 768], P('fsdp', 'ctx'), may hold values from -6 to 6
Outputs:
- output: float32 [4, 6144, 768], P('fsdp', 'ctx')
- grad_tokens: float32 [4, 6144, 768], P('fsdp', 'ctx')
- grad_query: float32 [768, 768], P('fsdp')
- grad_key: float32 [768, 768], P('fsdp')
- grad_value: float32 [768, 768], P('fsdp')
- grad_mixer: float32 [768, 768], P('fsdp')
- grad_inner: float32 [768, 3072], P('fsdp')
- grad_inbias: float32 [3072], P('fsdp')
- grad_outer: float32 [3072, 768], P('fsdp')
- grad_outbias: float32 [768], P('fsdp')
- grad_gain_one: float32 [768], P('fsdp')
- grad_shift_one: float32 [768], P('fsdp')
- grad_gain_two: float32 [768], P('fsdp')
- grad_shift_two: float32 [768], P('fsdp')
The draws below stay inside these ranges and needn't reach their ends.
Inputs may be any that keep to these rules, and one draw needn't show every extreme that they name: `seq_lengths`: one slot is full in every draw.
All inputs are finite; a program needn't handle non-finite values.
Results may differ from the reference program's by a relative error of at most 0.0014.
Values sent between devices are 32-bit elements; how exact they have to be, the bound alone decides.
No kernel may reach another device: no remote copies, remote signals or barrier semaphores. Data moves between devices by JAX's collectives and lax.ppermute only.
A program may use at most 576 MiB of HBM per device.

```python
import math
import jax
import jax.numpy as jnp
import numpy as np
from jax import lax

D = 768
H = 12
HD = 64
FF = 3072
SPAN = 64
SLOT_DEV = 384
SEQ = 6144
SLOTS = 4
N_CTX = 16


def touch_ends(values, own_key, smallest, top_value):
    dims = values.shape
    spot = [jax.random.randint(jax.random.fold_in(own_key, axis), (), 0, dims[axis]) for axis in range(len(dims))]
    values = values.at[tuple(spot)].set(smallest)
    longest = dims.index(max(dims))
    spot[longest] = (spot[longest] + 1) % dims[longest]
    return values.at[tuple(spot)].set(top_value)


def block_scale(own_key, dims, pieces, smallest, largest):
    level = 1.0
    for dim, blocks in pieces:
        heights = jax.random.uniform(jax.random.fold_in(jax.random.fold_in(own_key, 6), dim), (blocks,), jnp.float32, smallest / len(pieces), largest / len(pieces))
        level = level * jnp.repeat(jnp.exp(heights), dims[dim] // blocks).reshape((-1,) + (1,) * (len(dims) - 1 - dim))
    return level


def length_profile(count, total, reach, slope):
    portions = [(1 << 20) // math.isqrt(grade ** slope) + 1 for grade in range(2, count + 1)]
    spare, counts = total - reach - (count - 1), [1] * (count - 1)
    while spare > 0:
        movable = [i for i in range(count - 1) if counts[i] < reach]
        mass, budget = sum([portions[i] for i in movable]), spare
        for i in movable:
            addition = min(reach - counts[i], max(1, budget * portions[i] // mass), spare)
            counts[i] = counts[i] + addition
            spare = spare - addition
    return np.array([reach] + counts)


def ragged(key, amount, total, most, skew):
    if amount == 2:
        one = jax.random.randint(key, (), max(1, total - most), min(most, total - 1) + 1)
        return jnp.stack([one, total - one])
    lengths = jnp.asarray(length_profile(amount, total, most, skew), jnp.int32)
    twos = (amount - 1) // 2
    source_of, sink = lengths[1:1 + 2 * twos:2], lengths[2:2 + 2 * twos:2]
    room = jnp.minimum(source_of - 1, most - sink)
    passed = jax.random.randint(jax.random.fold_in(key, 1), (twos,), 0, 1 << 20) % (room + 1)
    lengths = lengths.at[1:1 + 2 * twos:2].set(source_of - passed).at[2:2 + 2 * twos:2].set(sink + passed)
    return lengths[jax.random.permutation(jax.random.fold_in(key, 2), amount)]


def noise(key, shape, width, limit, shards=(), held_as=jnp.bfloat16):
    values = width * jax.random.normal(key, shape, jnp.float32)
    if shards:
        values = values * block_scale(key, shape, shards, -0.22, 0.18)
    return jnp.clip(values, -limit, limit).astype(held_as)


def setup_inputs(seed: int = 0) -> dict:
    key_list = jax.random.split(jax.random.key(seed), 17)
    tokens = noise(key_list[0], (SLOTS, SEQ, D), 1.0, 6.0, ((0, 2), (1, 16)), jnp.float32)
    w_query = noise(key_list[1], (D, D), D ** -0.5, 0.21875, ((0, 2),), jnp.float32)
    w_key = noise(key_list[2], (D, D), D ** -0.5, 0.21875, ((0, 2),), jnp.float32)
    w_value = noise(key_list[3], (D, D), D ** -0.5, 0.21875, ((0, 2),), jnp.float32)
    w_mixer = noise(key_list[4], (D, D), (max(D // 256, 1)) ** -0.5, 3.5, ((0, 2),), jnp.float32)
    w_inner = noise(key_list[5], (D, FF), D ** -0.5, 0.21875, ((0, 2),), jnp.float32)
    b_inner = noise(key_list[6], (FF,), 0.5, 3.0, ((0, 2),), jnp.float32)
    w_outer = noise(key_list[7], (FF, D), FF ** -0.5, 0.109375, ((0, 2),), jnp.float32)
    b_outer = noise(key_list[8], (D,), 0.5, 3.0, ((0, 2),), jnp.float32)
    gain_one = jnp.clip(1.0 + 0.1 * jax.random.normal(key_list[9], (D,), jnp.float32), 0.5, 1.5)
    shift_one = noise(key_list[10], (D,), 0.5, 3.0, ((0, 2),), jnp.float32)
    gain_two = jnp.clip(1.0 + 0.1 * jax.random.normal(key_list[11], (D,), jnp.float32), 0.5, 1.5)
    shift_two = noise(key_list[12], (D,), 0.5, 3.0, ((0, 2),), jnp.float32)
    seq_lengths = ragged(key_list[13], SLOTS, SEQ * SLOTS // 2, SEQ, 1).astype(jnp.int32)
    rotation = touch_ends(jax.random.randint(key_list[14], (SLOTS,), 0, SEQ // SLOT_DEV), jax.random.fold_in(key_list[14], 1), 0, (SEQ // SLOT_DEV) - 1).astype(jnp.int32)
    cotangent = noise(key_list[15], (SLOTS, SEQ, D), 1.0, 6.0, ((0, 2), (1, 16)), jnp.float32)
    return {"tokens": tokens, "w_query": w_query, "w_key": w_key, "w_value": w_value, "w_mixer": w_mixer, "w_inner": w_inner, "b_inner": b_inner, "w_outer": w_outer, "b_outer": b_outer, "gain_one": gain_one, "shift_one": shift_one, "gain_two": gain_two, "shift_two": shift_two, "seq_lengths": seq_lengths, "rotation": rotation, "cotangent": cotangent}


HIGHEST = lax.Precision.HIGHEST

@jax.custom_vjp
def low(v):
    return lax.optimization_barrier(v.astype(jnp.bfloat16)).astype(jnp.float32)

@jax.custom_vjp
def low_back(v):
    return v

def low_keep(v):
    return (low(v), None)

def low_pass(kept, grad):
    return (grad,)

def back_keep(v):
    return (v, None)

def back_low(kept, grad):
    return (low(grad),)
low.defvjp(low_keep, low_pass)
low_back.defvjp(back_keep, back_low)

def matmul(left, right):
    return jnp.dot(left, right, precision=HIGHEST, preferred_element_type=jnp.float32)

def layer_norm(values, gain, shift):
    center = values - lax.optimization_barrier(jnp.mean(values, axis=-1, keepdims=True))
    spread = lax.optimization_barrier(jnp.mean(center * center, axis=-1, keepdims=True))
    return center * lax.rsqrt(spread + 1e-05) * gain + shift

def dealt_places(shift_by):
    row_ids = jnp.arange(SEQ, dtype=jnp.int32)
    device = row_ids // SLOT_DEV
    within = row_ids % SLOT_DEV
    pair_count = SLOT_DEV // (2 * SPAN)
    blocks = within // SPAN
    offset = within % SPAN
    group_id = (device + shift_by) % N_CTX
    span_count = SEQ // SPAN
    span_at = jnp.where(blocks < pair_count, group_id * pair_count + blocks, span_count - 1 - (group_id * pair_count + blocks - pair_count))
    return (span_at * SPAN + offset).astype(jnp.int32)

def features(projected, seq_len):
    places = jnp.arange(SEQ, dtype=jnp.int32)
    valid_rows = (places < seq_len).astype(jnp.float32)
    angles = 0.5 * math.pi * places.astype(jnp.float32) / seq_len.astype(jnp.float32)
    rectified = jnp.maximum(projected, 0.0).reshape(SEQ, H, HD)
    weight_cos = (jnp.cos(angles) * valid_rows)[:, None, None]
    weight_sin = (jnp.sin(angles) * valid_rows)[:, None, None]
    return jnp.concatenate([rectified * weight_cos, rectified * weight_sin], axis=-1)

def slot_layer(rows_in, seq_len, query_in, key_in, value_in, mixer_in, inner_in, inbias_in, outer_in, outbias_in, gain_first, shift_first, gain_second, shift_second):
    feat_query = features(matmul(rows_in, query_in), seq_len)
    feat_key = features(matmul(rows_in, key_in), seq_len)
    values = matmul(rows_in, value_in).reshape(SEQ, H, HD)
    augmented = jnp.concatenate([values, jnp.ones((SEQ, H, 1), jnp.float32)], axis=-1)
    block_count = SEQ // SPAN
    query_blocks = feat_query.reshape(block_count, SPAN, H, 2 * HD)
    key_blocks = feat_key.reshape(block_count, SPAN, H, 2 * HD)
    value_blocks = augmented.reshape(block_count, SPAN, H, HD + 1)
    causal = (jnp.arange(SPAN)[None, :] <= jnp.arange(SPAN)[:, None]).astype(jnp.float32)

    def advance(state, block):
        query_b, key_b, value_b = block
        scores = jnp.einsum('ihm,jhm->hij', query_b, key_b, precision=HIGHEST) * causal
        within_block = jnp.einsum('hij,jhv->ihv', scores, value_b, precision=HIGHEST)
        across = jnp.einsum('ihm,hvm->ihv', query_b, state, precision=HIGHEST)
        new_state = state + jnp.einsum('jhv,jhm->hvm', value_b, key_b, precision=HIGHEST)
        return (new_state, within_block + across)
    start_state = jnp.zeros((H, HD + 1, 2 * HD), jnp.float32)
    final_state, totals = lax.scan(jax.checkpoint(advance), start_state, (query_blocks, key_blocks, value_blocks))
    totals = totals.reshape(SEQ, H, HD + 1)
    attended = (totals[..., :HD] / jnp.maximum(totals[..., HD:], 1.0)).reshape(SEQ, D)
    hidden = layer_norm(rows_in + matmul(attended, mixer_in), gain_first, shift_first)
    activated = jax.nn.gelu(matmul(hidden, inner_in) + inbias_in, approximate=False)
    valid_rows = (jnp.arange(SEQ, dtype=jnp.int32) < seq_len).astype(jnp.float32)
    return valid_rows[:, None] * layer_norm(hidden + matmul(activated, outer_in) + outbias_in, gain_second, shift_second)

def reference(tokens, w_query, w_key, w_value, w_mixer, w_inner, b_inner, w_outer, b_outer, gain_one, shift_one, gain_two, shift_two, seq_lengths, rotation, cotangent):

    def forward(tokens_in, *params):
        results = []
        for slot in range(SLOTS):
            places = dealt_places(rotation[slot])
            ordered = jnp.zeros((SEQ,), jnp.int32).at[places].set(jnp.arange(SEQ, dtype=jnp.int32))
            natural = tokens_in[slot][ordered]
            result = slot_layer(natural, seq_lengths[slot], *params)
            results.append(result[places])
        return jnp.stack(results)
    output, pullback = jax.vjp(forward, tokens, w_query, w_key, w_value, w_mixer, w_inner, b_inner, w_outer, b_outer, gain_one, shift_one, gain_two, shift_two)
    grads = pullback(cotangent)
    return (output, grads[0], grads[1], grads[2], grads[3], grads[4], grads[5], grads[6], grads[7], grads[8], grads[9], grads[10], grads[11], grads[12])
```

```python
import functools
import math

import jax
import jax.numpy as jnp
from jax import lax
from jax.experimental import pallas as pl
from jax.experimental.pallas import tpu as pltpu
from jax.sharding import PartitionSpec as P

HEADS = 12
SPAN = 64
LANES = 128
FULL = lax.Precision.HIGHEST
TRIPLE = lax.Precision.HIGH
VMEM_BYTES = 56 * 1024 * 1024
NN = (((1,), (0,)), ((), ()))
NT = (((1,), (1,)), ((), ()))
TN = (((0,), (0,)), ((), ()))


def mul(left, right, dims=NN, precision=TRIPLE):
    return lax.dot_general(left, right, dims, precision=precision, preferred_element_type=jnp.float32)


def flip(bit, size):
    return [(place, place ^ (1 << bit)) for place in range(size)]


class Place:
    def __init__(self):
        self.size = lax.axis_size("ctx")
        self.index = lax.axis_index("ctx")
        self.pair = lax.axis_index("fsdp")
        self.bits = self.size.bit_length() - 1

    def bit(self, axis):
        return self.pair if axis == "fsdp" else (self.index >> axis) & 1

    def swap(self, value, axis):
        if axis == "fsdp":
            return lax.ppermute(value, "fsdp", [(0, 1), (1, 0)])
        return lax.ppermute(value, "ctx", flip(axis, self.size))


def in_order(bit, mine, other):
    return jnp.where(
        bit == 0, jnp.concatenate([mine, other], axis=0), jnp.concatenate([other, mine], axis=0)
    )


def whole_weight(place, shard):
    rows = shard.shape[0]
    quarter = rows // 4
    part = place.bit(0) * 2 + place.bit(1)
    first = place.swap(lax.dynamic_slice_in_dim(shard, part * quarter, quarter, 0), "fsdp")
    second = place.swap(first, 1)
    half = in_order(place.bit(1), first, second)
    other = in_order(place.bit(0), half, place.swap(half, 0))
    return in_order(place.pair, shard, other)


def halves(parts, bit, axis):
    size = parts[0].shape[axis] // 2
    take = lambda start: functools.reduce(
        jnp.add, [lax.dynamic_slice_in_dim(part, start * size, size, axis) for part in parts]
    )
    return take(bit), take(1 - bit)


def summed_gradient(place, grad):
    rows, columns = grad.shape
    middle = grad.reshape(2, 2, rows // 4, columns)
    core = place.bit(0)
    keep = lax.dynamic_index_in_dim(middle, core, 1, False)
    got = place.swap(lax.dynamic_index_in_dim(middle, 1 - core, 1, False), 0)
    rest = list(range(3, place.bits))
    orders = (["fsdp", 1, 2] + rest, [1, "fsdp", 2] + rest, [2, "fsdp", 1] + rest)
    width = columns // 3
    pieces = []
    for number, order in enumerate(orders):
        columns_of = slice(number * width, (number + 1) * width)
        parts = [keep[..., columns_of], got[..., columns_of]]
        for axis in order:
            stay, leave = halves(parts, place.bit(axis), 0 if axis == "fsdp" else 1)
            parts = [stay, place.swap(leave, axis)]
        piece = (parts[0] + parts[1])[0]
        for axis in reversed([axis for axis in order if axis != "fsdp"]):
            piece = in_order(place.bit(axis), piece, place.swap(piece, axis))
        pieces.append(piece)
    half = jnp.concatenate(pieces, axis=1)
    return in_order(core, half, place.swap(half, 0))


def params(semantics=1):
    return pltpu.CompilerParams(
        dimension_semantics=("arbitrary",) * semantics, vmem_limit_bytes=VMEM_BYTES
    )


def cost(flops, bytes_accessed):
    return pl.CostEstimate(flops=int(flops), bytes_accessed=int(bytes_accessed), transcendentals=0)


def lane_of(shape):
    return lax.broadcasted_iota(jnp.int32, shape, len(shape) - 1)


def first_head(shape):
    return (lane_of(shape) % LANES) < (LANES // 2)


def pair_state(values, weights, pair, feature, scratch):
    both = values[:, pair * LANES : (pair + 1) * LANES]
    product = mul(both, feature, TN)
    head = LANES // 2
    scratch[pair * head : (pair + 1) * head, :] = jnp.where(
        first_head((head, 2 * LANES)), product[:head], product[head:]
    )
    rows = feature.shape[0]
    if weights is not None:
        one = jnp.broadcast_to(weights[:, 2 * pair : 2 * pair + 1], (rows, 2 * LANES))
        two = jnp.broadcast_to(weights[:, 2 * pair + 1 : 2 * pair + 2], (rows, 2 * LANES))
        feature = feature * jnp.where(first_head((rows, 2 * LANES)), one, two)
    return jnp.sum(feature, axis=0, keepdims=True)


def store_state(scratch, ones, out_ref):
    pairs = len(ones)
    base = pairs * (LANES // 2)
    total = scratch.shape[0]
    tail = total - base
    row = lax.broadcasted_iota(jnp.int32, (tail, 2 * LANES), 0)
    block = jnp.zeros((tail, 2 * LANES), jnp.float32)
    for pair, line in enumerate(ones):
        block = jnp.where(row == pair, jnp.broadcast_to(line, block.shape), block)
    scratch[base:, :] = block
    step = out_ref.shape[3]
    for part in range(out_ref.shape[1]):
        out_ref[0, part, 0] = scratch[part * step : (part + 1) * step, :]


def load_state(state_ref, scratch):
    step = state_ref.shape[3]
    for part in range(state_ref.shape[1]):
        scratch[part * step : (part + 1) * step, :] = state_ref[0, part, 0]


def pair_matrix(scratch, pair, pairs):
    head = LANES // 2
    rows = scratch[pair * head : (pair + 1) * head, :]
    first = first_head((head, 2 * LANES))
    upper = jnp.where(first, rows, 0.0)
    lower = jnp.where(first, 0.0, rows)
    line = scratch[pairs * head + pair : pairs * head + pair + 1, :]
    row = lax.broadcasted_iota(jnp.int32, (LANES, 2 * LANES), 0)
    spread = jnp.broadcast_to(line, (LANES, 2 * LANES))
    first = first_head((LANES, 2 * LANES))
    last = jnp.where((row == 0) & first, spread, 0.0) + jnp.where((row == 1) & ~first, spread, 0.0)
    return jnp.concatenate([upper, lower, last], axis=0)


def angles(trig_ref, rows):
    wide = (rows, LANES)
    return (
        jnp.broadcast_to(trig_ref[:, 0:1], wide),
        jnp.broadcast_to(trig_ref[:, 1:2], wide),
    )


def state_kernel(key_ref, value_ref, trig_ref, out_ref, scratch):
    rows = key_ref.shape[0]
    cos, sin = angles(trig_ref, rows)
    ones = []
    for pair in range(key_ref.shape[1] // LANES):
        key = key_ref[:, pair * LANES : (pair + 1) * LANES]
        feature = jnp.concatenate([key * cos, key * sin], axis=1)
        ones.append(pair_state(value_ref, None, pair, feature, scratch))
    store_state(scratch, ones, out_ref)


def attend_kernel(query_ref, key_ref, value_ref, trig_ref, gate_ref, state_ref, out_ref, den_ref, scratch):
    rows, width = query_ref.shape
    pairs = width // LANES
    cos, sin = angles(trig_ref, rows)
    gate = gate_ref[0]
    load_state(state_ref, scratch)
    first = first_head((rows, LANES))
    lane = lane_of((rows, LANES))
    dens = jnp.zeros((rows, LANES), jnp.float32)
    for pair in range(pairs):
        at = slice(pair * LANES, (pair + 1) * LANES)
        query, key, value = query_ref[:, at], key_ref[:, at], value_ref[:, at]
        feature = jnp.concatenate([query * cos, query * sin], axis=1)
        total = mul(feature, pair_matrix(scratch, pair, pairs), NT)
        marks, scores = [], []
        for head in range(2):
            own = first if head == 0 else ~first
            scores.append(mul(jnp.where(own, query, 0.0), key, NT) * gate)
            marks.append(
                jnp.concatenate(
                    [jnp.where(own, value, 0.0), jnp.where(lane == head, 1.0, 0.0)], axis=1
                )
            )
        total = total + mul(scores[0], marks[0]) + mul(scores[1], marks[1])
        num, den = total[:, :LANES], total[:, LANES:]
        one = jnp.broadcast_to(den[:, 0:1], (rows, LANES))
        two = jnp.broadcast_to(den[:, 1:2], (rows, LANES))
        out_ref[:, at] = num / jnp.maximum(jnp.where(first, one, two), 1.0)
        dens = jnp.where(lane == 2 * pair, one, jnp.where(lane == 2 * pair + 1, two, dens))
    den_ref[...] = dens


def back_state_kernel(da_ref, attended_ref, den_ref, query_ref, trig_ref, dtot_ref, dden_ref, out_ref, scratch):
    rows, width = query_ref.shape
    cos, sin = angles(trig_ref, rows)
    first = first_head((rows, LANES))
    lane = lane_of((rows, LANES))
    ddens = jnp.zeros((rows, LANES), jnp.float32)
    for pair in range(width // LANES):
        at = slice(pair * LANES, (pair + 1) * LANES)
        grad = da_ref[:, at]
        both = grad * attended_ref[:, at]
        for head in range(2):
            column = 2 * pair + head
            own = first if head == 0 else ~first
            den = den_ref[:, column : column + 1]
            part = jnp.sum(jnp.where(own, both, 0.0), axis=1, keepdims=True)
            change = jnp.where(den > 1.0, -part / jnp.maximum(den, 1.0), 0.0)
            ddens = jnp.where(lane == column, jnp.broadcast_to(change, (rows, LANES)), ddens)
        one = jnp.broadcast_to(den_ref[:, 2 * pair : 2 * pair + 1], (rows, LANES))
        two = jnp.broadcast_to(den_ref[:, 2 * pair + 1 : 2 * pair + 2], (rows, LANES))
        dtot_ref[:, at] = grad / jnp.maximum(jnp.where(first, one, two), 1.0)
    dden_ref[...] = ddens
    ones = []
    for pair in range(width // LANES):
        query = query_ref[:, pair * LANES : (pair + 1) * LANES]
        feature = jnp.concatenate([query * cos, query * sin], axis=1)
        ones.append(pair_state(dtot_ref, ddens, pair, feature, scratch))
    store_state(scratch, ones, out_ref)


def back_attend_kernel(
    query_ref, key_ref, value_ref, dtot_ref, dden_ref, trig_ref, gate_ref, state_ref, grad_ref,
    dquery_ref, dkey_ref, dvalue_ref, scratch, grad_scratch,
):
    rows, width = query_ref.shape
    pairs = width // LANES
    cos, sin = angles(trig_ref, rows)
    gate = gate_ref[0]
    load_state(state_ref, scratch)
    load_state(grad_ref, grad_scratch)
    first = first_head((rows, LANES))
    lane = lane_of((rows, LANES))
    for pair in range(pairs):
        at = slice(pair * LANES, (pair + 1) * LANES)
        query, key, value, dtot = query_ref[:, at], key_ref[:, at], value_ref[:, at], dtot_ref[:, at]
        drops = [dden_ref[:, 2 * pair + head : 2 * pair + head + 1] for head in range(2)]
        weight = jnp.where(
            lane == 0,
            jnp.broadcast_to(drops[0], (rows, LANES)),
            jnp.where(lane == 1, jnp.broadcast_to(drops[1], (rows, LANES)), 0.0),
        )
        before = mul(jnp.concatenate([dtot, weight], axis=1), pair_matrix(scratch, pair, pairs))
        dquery = before[:, :LANES] * cos + before[:, LANES:] * sin
        after = pair_matrix(grad_scratch, pair, pairs)
        counted = jnp.concatenate([value, jnp.where(lane < 2, 1.0, 0.0)], axis=1)
        onward = mul(counted, after)
        dkey = onward[:, :LANES] * cos + onward[:, LANES:] * sin
        feature = jnp.concatenate([key * cos, key * sin], axis=1)
        dvalue = mul(feature, after, NT)[:, :LANES]
        for head in range(2):
            own = first if head == 0 else ~first
            query_own = jnp.where(own, query, 0.0)
            dtot_own = jnp.where(own, dtot, 0.0)
            scores = mul(query_own, key, NT) * gate
            back = (mul(dtot_own, value, NT) + drops[head]) * gate
            dquery = dquery + mul(back, jnp.where(own, key, 0.0))
            dkey = dkey + mul(back, query_own, TN)
            dvalue = dvalue + mul(scores, dtot_own, TN)
        dquery_ref[:, at] = jnp.where(query > 0.0, dquery, 0.0)
        dkey_ref[:, at] = jnp.where(key > 0.0, dkey, 0.0)
        dvalue_ref[:, at] = dvalue


def scan_kernel(shift_ref, states_ref, out_ref, *, reverse):
    size = states_ref.shape[0]
    shift = shift_ref[0]

    def step(number, running):
        spot = 2 * size - 1 - number if reverse else number
        late = spot >= size
        group = jnp.where(late, 2 * size - 1 - spot, spot)
        device = lax.rem(group - shift + size, size)
        half = late.astype(jnp.int32)
        out_ref[device, half] = running
        return running + states_ref[device, half]

    lax.fori_loop(0, 2 * size, step, jnp.zeros(states_ref.shape[2:], jnp.float32))


def scan_states(place, states, rotation, reverse):
    slots, parts, two, rows, width = states.shape
    flat = states.reshape(slots * parts, two, rows, width)
    gathered = lax.all_to_all(flat, "ctx", 0, 0, tiled=True)
    shift = lax.dynamic_slice_in_dim(rotation, place.index // parts, 1)
    summed = pl.pallas_call(
        functools.partial(scan_kernel, reverse=reverse),
        grid_spec=pltpu.PrefetchScalarGridSpec(
            num_scalar_prefetch=1,
            grid=(1,),
            in_specs=[pl.BlockSpec(gathered.shape, lambda i, s: (0, 0, 0, 0))],
            out_specs=pl.BlockSpec(gathered.shape, lambda i, s: (0, 0, 0, 0)),
        ),
        out_shape=jax.ShapeDtypeStruct(gathered.shape, jnp.float32),
        compiler_params=params(),
        cost_estimate=cost(gathered.size, 8 * gathered.size),
        name="scan_states",
    )(shift, gathered)
    back = lax.all_to_all(summed, "ctx", 0, 0, tiled=True)
    return back.reshape(states.shape)


def normalize(values):
    center = values - jnp.mean(values, axis=-1, keepdims=True)
    spread = jnp.mean(center * center, axis=-1, keepdims=True)
    root = lax.rsqrt(spread + 1e-05)
    return center * root, root


def back_normalize(grad, normal, root):
    return (
        grad
        - jnp.mean(grad, axis=-1, keepdims=True)
        - normal * jnp.mean(grad * normal, axis=-1, keepdims=True)
    ) * root


def per_device(
    tokens, w_query, w_key, w_value, w_mixer, w_inner, b_inner, w_outer, b_outer,
    gain_one, shift_one, gain_two, shift_two, seq_lengths, rotation, cotangent,
):
    place = Place()
    slots, slot_rows, width = tokens.shape
    rows = slots * slot_rows
    half_rows = slot_rows // 2
    chunks = slots * 2
    heads = HEADS
    pairs = heads // 2
    parts = place.size // slots
    state_rows = pairs * (LANES // 2) + pairs
    step = -(-state_rows // parts)
    step = -(-step // 8) * 8
    state_shape = (slots, parts, 2, step, 2 * LANES)

    first_slot = place.pair * slots
    lengths = lax.dynamic_slice_in_dim(seq_lengths, first_slot, slots)
    turns = lax.dynamic_slice_in_dim(rotation, first_slot, slots)
    group = (place.index + turns) % place.size
    within = jnp.arange(slot_rows, dtype=jnp.int32)
    per_group = half_rows // SPAN
    block = within // SPAN
    spans = place.size * 2 * per_group
    early = group[:, None] * per_group + block[None, :]
    late = spans - 1 - (group[:, None] * per_group + block[None, :] - per_group)
    spot = jnp.where(block[None, :] < per_group, early, late) * SPAN + (within % SPAN)[None, :]
    valid = (spot < lengths[:, None]).astype(jnp.float32)
    angle = 0.5 * math.pi * spot.astype(jnp.float32) / lengths[:, None].astype(jnp.float32)
    cos, sin = jnp.cos(angle) * valid, jnp.sin(angle) * valid
    trig = jnp.pad(jnp.stack([cos, sin], axis=-1).reshape(rows, 2), ((0, 0), (0, LANES - 2)))
    cut = lambda array: array.reshape(chunks, half_rows)
    pos, cos_cut, sin_cut = cut(spot), cut(cos), cut(sin)
    gate = jnp.where(
        pos[:, None, :] <= pos[:, :, None],
        cos_cut[:, :, None] * cos_cut[:, None, :] + sin_cut[:, :, None] * sin_cut[:, None, :],
        0.0,
    )
    valid = valid.reshape(rows, 1)

    vectors = jnp.concatenate([b_inner, b_outer, gain_one, shift_one, gain_two, shift_two])
    other_vectors = place.swap(vectors, "fsdp")
    key_in = whole_weight(place, w_key)
    value_in = whole_weight(place, w_value)
    query_in = whole_weight(place, w_query)
    w_mixer, w_inner, w_outer, _ = lax.optimization_barrier((w_mixer, w_inner, w_outer, other_vectors))
    mixer_in = whole_weight(place, w_mixer)
    inner_in = whole_weight(place, w_inner)
    outer_in = whole_weight(place, w_outer)
    sizes = [b_inner.shape[0]] + [width // 2] * 5
    mine, others, offset = [], [], 0
    for size in sizes:
        mine.append(vectors[offset : offset + size])
        others.append(other_vectors[offset : offset + size])
        offset += size
    bias_in, bias_out, gain_first, shift_first, gain_second, shift_second = [
        in_order(place.pair, own, other) for own, other in zip(mine, others)
    ]

    flat = tokens.reshape(rows, width)
    key = jnp.maximum(mul(flat, key_in, precision=FULL), 0.0)
    value = mul(flat, value_in)
    query = jnp.maximum(mul(flat, query_in, precision=FULL), 0.0)

    row_spec = pl.BlockSpec((half_rows, width), lambda i: (i, 0))
    lane_spec = pl.BlockSpec((half_rows, LANES), lambda i: (i, 0))
    gate_spec = pl.BlockSpec((1, half_rows, half_rows), lambda i: (i, 0, 0))
    state_spec = pl.BlockSpec(
        (1, parts, 1, step, 2 * LANES), lambda i: (lax.div(i, 2), 0, lax.rem(i, 2), 0, 0)
    )
    row_type = jax.ShapeDtypeStruct((rows, width), jnp.float32)
    lane_type = jax.ShapeDtypeStruct((rows, LANES), jnp.float32)
    state_type = jax.ShapeDtypeStruct(state_shape, jnp.float32)
    state_scratch = pltpu.VMEM((parts * step, 2 * LANES), jnp.float32)

    states = pl.pallas_call(
        state_kernel,
        grid=(chunks,),
        in_specs=[row_spec, row_spec, lane_spec],
        out_specs=state_spec,
        out_shape=state_type,
        scratch_shapes=[state_scratch],
        compiler_params=params(),
        cost_estimate=cost(2e9, 8e6),
        name="key_states",
    )(key, value, trig)
    before = scan_states(place, states, turns, False)
    attended, den = pl.pallas_call(
        attend_kernel,
        grid=(chunks,),
        in_specs=[row_spec, row_spec, row_spec, lane_spec, gate_spec, state_spec],
        out_specs=[row_spec, lane_spec],
        out_shape=[row_type, lane_type],
        scratch_shapes=[state_scratch],
        compiler_params=params(),
        cost_estimate=cost(6e9, 12e6),
        name="attend",
    )(query, key, value, trig, gate, before)

    normal_one, root_one = normalize(flat + mul(attended, mixer_in))
    hidden = normal_one * gain_first + shift_first
    inner = mul(hidden, inner_in) + bias_in
    phi_sum = 0.5 * lax.erfc(-inner * math.sqrt(0.5))
    activated = inner * phi_sum
    slope = phi_sum + inner * (jnp.exp(-0.5 * inner * inner) * (1.0 / math.sqrt(2.0 * math.pi)))
    normal_two, root_two = normalize(hidden + mul(activated, outer_in) + bias_out)
    output = valid * (normal_two * gain_second + shift_second)

    err_two = valid * cotangent.reshape(rows, width)
    grad_gain_two = jnp.sum(err_two * normal_two, axis=0)
    grad_shift_two = jnp.sum(err_two, axis=0)
    rest_two = back_normalize(err_two * gain_second, normal_two, root_two)
    grad_outer = mul(activated, rest_two, TN)
    grad_outbias = jnp.sum(rest_two, axis=0)
    dinner = mul(rest_two, outer_in, NT) * slope
    grad_inner = mul(hidden, dinner, TN)
    grad_inbias = jnp.sum(dinner, axis=0)
    err_one = rest_two + mul(dinner, inner_in, NT)
    grad_gain_one = jnp.sum(err_one * normal_one, axis=0)
    grad_shift_one = jnp.sum(err_one, axis=0)
    rest_one = back_normalize(err_one * gain_first, normal_one, root_one)
    grad_mixer = mul(attended, rest_one, TN)
    dattended = mul(rest_one, mixer_in, NT)

    dtot, dden, back_states = pl.pallas_call(
        back_state_kernel,
        grid=(chunks,),
        in_specs=[row_spec, row_spec, lane_spec, row_spec, lane_spec],
        out_specs=[row_spec, lane_spec, state_spec],
        out_shape=[row_type, lane_type, state_type],
        scratch_shapes=[state_scratch],
        compiler_params=params(),
        cost_estimate=cost(2e9, 12e6),
        name="query_states",
    )(dattended, attended, den, query, trig)
    after = scan_states(place, back_states, turns, True)
    dquery, dkey, dvalue = pl.pallas_call(
        back_attend_kernel,
        grid=(chunks,),
        in_specs=[row_spec] * 4 + [lane_spec, lane_spec, gate_spec, state_spec, state_spec],
        out_specs=[row_spec] * 3,
        out_shape=[row_type] * 3,
        scratch_shapes=[state_scratch] * 2,
        compiler_params=params(),
        cost_estimate=cost(12e9, 24e6),
        name="back_attend",
    )(query, key, value, dtot, dden, trig, gate, before, after)
    grad_query = mul(flat, dquery, TN)
    grad_key = mul(flat, dkey, TN)
    grad_value = mul(flat, dvalue, TN)
    grad_tokens = rest_one + mul(dquery, query_in, NT) + mul(dkey, key_in, NT) + mul(dvalue, value_in, NT)

    small = lax.psum(
        jnp.concatenate(
            [grad_inbias, grad_outbias, grad_gain_one, grad_shift_one, grad_gain_two, grad_shift_two]
        ),
        ("ctx", "fsdp"),
    )
    narrow, offset = [], 0
    for size in sizes:
        narrow.append(lax.dynamic_slice_in_dim(small, offset + place.pair * size, size))
        offset += 2 * size
    grad_inbias, grad_outbias, grad_gain_one, grad_shift_one, grad_gain_two, grad_shift_two = narrow
    return (
        output.reshape(tokens.shape),
        grad_tokens.reshape(tokens.shape),
        summed_gradient(place, grad_query),
        summed_gradient(place, grad_key),
        summed_gradient(place, grad_value),
        summed_gradient(place, grad_mixer),
        summed_gradient(place, grad_inner),
        grad_inbias,
        summed_gradient(place, grad_outer),
        grad_outbias,
        grad_gain_one,
        grad_shift_one,
        grad_gain_two,
        grad_shift_two,
    )


def solution(mesh):
    rows = P("fsdp", "ctx", None)
    matrix = P("fsdp", None)
    vector = P("fsdp")
    in_specs = (
        rows, matrix, matrix, matrix, matrix, matrix, vector, matrix, vector,
        vector, vector, vector, vector, P(), P(), rows,
    )
    out_specs = (
        rows, rows, matrix, matrix, matrix, matrix, matrix, vector, matrix,
        vector, vector, vector, vector, vector,
    )
    return jax.shard_map(
        per_device, mesh=mesh, in_specs=in_specs, out_specs=out_specs, check_vma=False
    )
```

```python
import functools
import math

import jax
import jax.numpy as jnp
from jax import lax
from jax.experimental import pallas as pl
from jax.experimental.pallas import tpu as pltpu
from jax.sharding import PartitionSpec as P

HEADS = 12
SPAN = 64
LANES = 128
FULL = lax.Precision.HIGHEST
TRIPLE = lax.Precision.HIGH
VMEM_BYTES = 56 * 1024 * 1024
NN = (((1,), (0,)), ((), ()))
NT = (((1,), (1,)), ((), ()))
TN = (((0,), (0,)), ((), ()))


def mul(left, right, dims=NN, precision=TRIPLE):
    return lax.dot_general(left, right, dims, precision=precision, preferred_element_type=jnp.float32)


def flip(bit, size):
    return [(place, place ^ (1 << bit)) for place in range(size)]


class Place:
    def __init__(self):
        self.size = lax.axis_size("ctx")
        self.index = lax.axis_index("ctx")
        self.pair = lax.axis_index("fsdp")
        self.bits = self.size.bit_length() - 1
        self.core = self.index & 1

    def bit(self, axis):
        return self.pair if axis == "fsdp" else (self.index >> axis) & 1

    def swap(self, value, axis):
        if axis == "fsdp":
            return lax.ppermute(value, "fsdp", [(0, 1), (1, 0)])
        return lax.ppermute(value, "ctx", flip(axis, self.size))


def in_order(bit, mine, other, axis=0):
    return jnp.where(
        bit == 0,
        jnp.concatenate([mine, other], axis=axis),
        jnp.concatenate([other, mine], axis=axis),
    )


def after(value, *others):
    return lax.optimization_barrier((value, *others))[0]


def fetch(place, shard, axis, *others):
    size = shard.shape[0] // 4
    part = 2 * place.core + place.bit(axis)
    leave = lax.dynamic_slice_in_dim(shard, part * size, size, 0)
    if others:
        leave = after(leave, *others)
    return place.swap(leave, "fsdp")


def sum_parts(parts, start, size, axis):
    return functools.reduce(
        jnp.add, [lax.dynamic_slice_in_dim(part, start, size, axis) for part in parts]
    )


class Reduction:
    def __init__(self, place, blocks):
        self.place = place
        rest = list(range(3, place.bits))
        self.orders = (["fsdp", 2, 1] + rest, [1, "fsdp", 2] + rest)
        size = blocks[0][0].shape[1] // 2
        self.parts = [
            [
                [lax.slice_in_dim(part, number * size, (number + 1) * size, axis=1) for part in block]
                for block in blocks
            ]
            for number in range(2)
        ]
        self.back = [[axis for axis in reversed(order) if axis != "fsdp"] for order in self.orders]
        self.pieces = None
        self.sent = []
        self.moves = self.moving()

    def moving(self):
        place = self.place
        for step in range(len(self.orders[0])):
            self.sent, stays, axes = [], [], []
            for number, order in enumerate(self.orders):
                axis = order[step]
                along = 0 if axis == "fsdp" else 1
                half = self.parts[number][0][0].shape[along] // 2
                bit = self.bit(axis)
                pack = lambda start: jnp.concatenate(
                    [sum_parts(block, start * half, half, along) for block in self.parts[number]], axis=-1
                )
                stays.append(pack(bit))
                self.sent.append(pack(1 - bit))
                axes.append(axis)
            self.parts = [
                [[stay, place.swap(leave, axis)]] for stay, leave, axis in zip(stays, self.sent, axes)
            ]
            yield
        self.pieces = [(self.late(block[0][0]) + block[0][1])[0] for block in self.parts]
        for step in range(len(self.back[0])):
            self.sent = self.pieces
            got = [place.swap(piece, axes[step]) for axes, piece in zip(self.back, self.pieces)]
            yield
            self.pieces = [
                in_order(self.bit(axes[step]), piece, other)
                for axes, piece, other in zip(self.back, self.pieces, got)
            ]

        mine = jnp.concatenate(self.pieces, axis=0)
        self.sent = [mine]
        self.result = (mine, place.swap(mine, 0))
        yield

    def late(self, value):
        return after(value, *self.others) if self.others else value

    def bit(self, axis):
        return self.late(self.place.bit(axis))

    def advance(self, *others):
        self.others = others
        next(self.moves)
        return self.sent


def advance_all(sums, others):
    return [sent for reduction in sums for sent in reduction.advance(*others)]


def join_kernel(core_ref, mine_ref, other_ref, out_ref):
    @pl.when(pl.program_id(0) == core_ref[0])
    def _():
        out_ref[...] = mine_ref[...]

    @pl.when(pl.program_id(0) != core_ref[0])
    def _():
        out_ref[...] = other_ref[...]


def join(core, mine, other, start, count, width, axis):
    rows = mine.shape[0]
    source = pl.BlockSpec((rows, width), lambda i, j, c: (0, start // width + j))
    place_of = (lambda i, j, c: (i * count + j, 0)) if axis == 0 else (lambda i, j, c: (0, i * count + j))
    shape = (2 * count * rows, width) if axis == 0 else (rows, 2 * count * width)
    return pl.pallas_call(
        join_kernel,
        grid_spec=pltpu.PrefetchScalarGridSpec(
            num_scalar_prefetch=1,
            grid=(2, count),
            in_specs=[source, source],
            out_specs=pl.BlockSpec((rows, width), place_of),
        ),
        out_shape=jax.ShapeDtypeStruct(shape, jnp.float32),
        compiler_params=params(2),
        cost_estimate=cost(0, 16 * rows * width * count),
        name="join",
    )(core, mine, other)


def params(semantics=1):
    return pltpu.CompilerParams(
        dimension_semantics=("arbitrary",) * semantics, vmem_limit_bytes=VMEM_BYTES
    )


def cost(flops, bytes_accessed):
    return pl.CostEstimate(flops=int(flops / 1000), bytes_accessed=int(bytes_accessed / 1000), transcendentals=0)


def lane_of(shape):
    return lax.broadcasted_iota(jnp.int32, shape, len(shape) - 1)


def first_head(shape):
    return (lane_of(shape) % LANES) < (LANES // 2)


def pair_state(values, weights, pair, feature, scratch):
    both = values[:, pair * LANES : (pair + 1) * LANES]
    product = mul(both, feature, TN)
    head = LANES // 2
    scratch[pair * head : (pair + 1) * head, :] = jnp.where(
        first_head((head, 2 * LANES)), product[:head], product[head:]
    )
    rows = feature.shape[0]
    if weights is not None:
        one = jnp.broadcast_to(weights[:, 2 * pair : 2 * pair + 1], (rows, 2 * LANES))
        two = jnp.broadcast_to(weights[:, 2 * pair + 1 : 2 * pair + 2], (rows, 2 * LANES))
        feature = feature * jnp.where(first_head((rows, 2 * LANES)), one, two)
    return jnp.sum(feature, axis=0, keepdims=True)


def store_state(scratch, ones, out_ref):
    pairs = len(ones)
    base = pairs * (LANES // 2)
    total = scratch.shape[0]
    tail = total - base
    row = lax.broadcasted_iota(jnp.int32, (tail, 2 * LANES), 0)
    block = jnp.zeros((tail, 2 * LANES), jnp.float32)
    for pair, line in enumerate(ones):
        block = jnp.where(row == pair, jnp.broadcast_to(line, block.shape), block)
    scratch[base:, :] = block
    step = out_ref.shape[3]
    for part in range(out_ref.shape[1]):
        out_ref[0, part, 0] = scratch[part * step : (part + 1) * step, :]


def load_state(info_ref, mine_ref, other_ref, scratch):
    step = mine_ref.shape[2]
    mine = lax.div(pl.program_id(0), 2) == info_ref[1]

    def load(state_ref):
        for part in range(state_ref.shape[0]):
            scratch[part * step : (part + 1) * step, :] = state_ref[part, 0]

    @pl.when(mine)
    def _():
        load(mine_ref)

    @pl.when(jnp.logical_not(mine))
    def _():
        load(other_ref)


def pair_matrix(scratch, pair, pairs):
    head = LANES // 2
    rows = scratch[pair * head : (pair + 1) * head, :]
    first = first_head((head, 2 * LANES))
    upper = jnp.where(first, rows, 0.0)
    lower = jnp.where(first, 0.0, rows)
    line = scratch[pairs * head + pair : pairs * head + pair + 1, :]
    row = lax.broadcasted_iota(jnp.int32, (LANES, 2 * LANES), 0)
    spread = jnp.broadcast_to(line, (LANES, 2 * LANES))
    first = first_head((LANES, 2 * LANES))
    last = jnp.where((row == 0) & first, spread, 0.0) + jnp.where((row == 1) & ~first, spread, 0.0)
    return jnp.concatenate([upper, lower, last], axis=0)


def angles(trig_ref, rows):
    wide = (rows, LANES)
    return (
        jnp.broadcast_to(trig_ref[:, 0:1], wide),
        jnp.broadcast_to(trig_ref[:, 1:2], wide),
    )


def load_weights(info_ref, groups, sems, first):
    pair = info_ref[0]
    for number, (own, pieces, start, axis, whole) in enumerate(groups):
        rows, size = own.shape[0], pieces[0].shape[0]
        part = 2 * info_ref[1] + info_ref[1 + axis]
        sources = [(own, pair * rows)]
        for turn, piece in enumerate(pieces):
            columns = piece.at[:, start : start + own.shape[1]]
            sources.append((columns, (1 - pair) * rows + (part ^ turn) * size))
        for piece, (source, row) in enumerate(sources):
            copy = pltpu.make_async_copy(
                source,
                whole.at[pl.ds(pl.multiple_of(row, 8), source.shape[0]), :],
                sems.at[number, piece],
            )
            copy.start() if first else copy.wait()


def chunk_valid(info_ref):
    return info_ref[4 + pl.program_id(0)] > 0


def zero(*refs):
    for ref in refs:
        ref[...] = jnp.zeros(ref.shape, ref.dtype)


def load_once(info_ref, groups, sems):
    @pl.when(pl.program_id(0) == 0)
    def _():
        load_weights(info_ref, groups, sems, True)
        load_weights(info_ref, groups, sems, False)


def key_kernel(
    info_ref, tokens_ref, trig_ref, key_own, value_own, one, two, three, four,
    key_ref, value_ref, out_ref, key_in, value_in, scratch, sems,
):
    load_once(
        info_ref,
        [
            (key_own, (one, two, three, four), 0, 1, key_in),
            (value_own, (one, two, three, four), key_own.shape[1], 1, value_in),
        ],
        sems,
    )
    valid = chunk_valid(info_ref)

    @pl.when(valid)
    def _():
        rows, width = tokens_ref.shape
        cos, sin = angles(trig_ref, rows)
        tokens = tokens_ref[...]
        key_ref[...] = jnp.maximum(mul(tokens, key_in[...], precision=FULL), 0.0)
        value_ref[...] = mul(tokens, value_in[...])
        ones = []
        for pair in range(width // LANES):
            key = key_ref[:, pair * LANES : (pair + 1) * LANES]
            feature = jnp.concatenate([key * cos, key * sin], axis=1)
            ones.append(pair_state(value_ref, None, pair, feature, scratch))
        store_state(scratch, ones, out_ref)

    @pl.when(jnp.logical_not(valid))
    def _():
        zero(key_ref, value_ref, out_ref)


def query_kernel(info_ref, tokens_ref, own, one, two, three, four, query_ref, query_in, sems):
    load_once(info_ref, [(own, (one, two, three, four), 0, 1, query_in)], sems)
    valid = chunk_valid(info_ref)

    @pl.when(valid)
    def _():
        query_ref[...] = jnp.maximum(mul(tokens_ref[...], query_in[...], precision=FULL), 0.0)

    @pl.when(jnp.logical_not(valid))
    def _():
        zero(query_ref)


def attend_kernel(
    info_ref, query_ref, key_ref, value_ref, trig_ref, gate_ref, state_ref, other_ref, out_ref, den_ref, scratch
):
    valid = chunk_valid(info_ref)

    @pl.when(jnp.logical_not(valid))
    def _():
        zero(out_ref, den_ref)

    @pl.when(valid)
    def _():
        rows, width = query_ref.shape
        pairs = width // LANES
        cos, sin = angles(trig_ref, rows)
        gate = gate_ref[0]
        load_state(info_ref, state_ref, other_ref, scratch)
        first = first_head((rows, LANES))
        lane = lane_of((rows, LANES))
        dens = jnp.zeros((rows, LANES), jnp.float32)
        for pair in range(pairs):
            at = slice(pair * LANES, (pair + 1) * LANES)
            query, key, value = query_ref[:, at], key_ref[:, at], value_ref[:, at]
            feature = jnp.concatenate([query * cos, query * sin], axis=1)
            total = mul(feature, pair_matrix(scratch, pair, pairs), NT)
            for head in range(2):
                own = first if head == 0 else ~first
                scores = mul(jnp.where(own, query, 0.0), key, NT) * gate
                marked = jnp.concatenate(
                    [jnp.where(own, value, 0.0), jnp.where(lane == head, 1.0, 0.0)], axis=1
                )
                total = total + mul(scores, marked)
            num, den = total[:, :LANES], total[:, LANES:]
            one = jnp.broadcast_to(den[:, 0:1], (rows, LANES))
            two = jnp.broadcast_to(den[:, 1:2], (rows, LANES))
            out_ref[:, at] = num / jnp.maximum(jnp.where(first, one, two), 1.0)
            dens = jnp.where(lane == 2 * pair, one, jnp.where(lane == 2 * pair + 1, two, dens))
        den_ref[...] = dens


def normalize(values):
    center = values - jnp.mean(values, axis=-1, keepdims=True)
    spread = jnp.mean(center * center, axis=-1, keepdims=True)
    root = lax.rsqrt(spread + 1e-05)
    return center * root, root


def back_normalize(grad, normal, root):
    return (
        grad
        - jnp.mean(grad, axis=-1, keepdims=True)
        - normal * jnp.mean(grad * normal, axis=-1, keepdims=True)
    ) * root


def normal_cdf(u):
    z = jnp.abs(u) * math.sqrt(0.5)
    t = 1.0 / (1.0 + 0.5 * z)
    series = 0.17087277
    for factor in (
        -0.82215223, 1.48851587, -1.13520398, 0.27886807, -0.18628806, 0.09678418, 0.37409196,
        1.00002368, -1.26551223,
    ):
        series = series * t + factor
    tail = 0.5 * t * jnp.exp(series - z * z)
    return jnp.where(u < 0.0, tail, 1.0 - tail), jnp.exp(-0.5 * u * u) * (1.0 / math.sqrt(2.0 * math.pi))


def layer_kernel(
    info_ref, tokens_ref, attended_ref, cot_ref, trig_ref, lines_ref, bias_ref,
    mixer_own, mixer_1, mixer_2, mixer_3, mixer_4, inner_own, inner_1, inner_2, inner_3, inner_4,
    outer_own, outer_1, outer_2, outer_3, outer_4,
    output_ref, hidden_ref, activated_ref, rest_two_ref, dinner_ref, rest_one_ref, dattended_ref,
    sums_ref, bias_sums_ref,
    mixer_in, inner_in, outer_in, slope_ref, normal_ref, root_ref, sems,
):
    width = tokens_ref.shape[1]
    groups = [
        (mixer_own, (mixer_1, mixer_2, mixer_3, mixer_4), width, 1, mixer_in),
        (inner_own, (inner_1, inner_2, inner_3, inner_4), 0, 1, inner_in),
        (outer_own, (outer_1, outer_2, outer_3, outer_4), 0, 2, outer_in),
    ]
    start = pl.program_id(0) == 0
    wait = lambda number: load_weights(
        info_ref, groups[number : number + 1], sems.at[number : number + 1], False
    )
    valid = chunk_valid(info_ref)
    rows = tokens_ref.shape[0]
    tiles = slope_ref.shape[1] // width
    line = lambda number: lines_ref[number : number + 1, :]
    total = lambda values: jnp.sum(values, axis=0, keepdims=True)

    @pl.when(start)
    def _():
        load_weights(info_ref, groups, sems, True)
        zero(sums_ref, bias_sums_ref)
        wait(0)

    @pl.when(jnp.logical_not(valid))
    def _():
        zero(output_ref, hidden_ref, activated_ref, rest_two_ref, dinner_ref, rest_one_ref, dattended_ref)

    @pl.when(valid)
    def _():
        normal_one, root_one = normalize(tokens_ref[...] + mul(attended_ref[...], mixer_in[...]))
        hidden = normal_one * line(1) + line(2)
        hidden_ref[...] = hidden
        normal_ref[...] = normal_one
        root_ref[...] = jnp.broadcast_to(root_one, root_ref.shape)

    @pl.when(start)
    def _():
        wait(1)
        wait(2)

    @pl.when(valid)
    def _():
        mask = jnp.broadcast_to(trig_ref[:, 2:3], (rows, width))
        hidden = hidden_ref[...]
        summed = hidden + line(0)
        for tile in range(tiles):
            at = slice(tile * width, (tile + 1) * width)
            u = mul(hidden, inner_in[:, at]) + bias_ref[0:1, at]
            below, density = normal_cdf(u)
            activated = u * below
            activated_ref[:, at] = activated
            slope_ref[:, at] = below + u * density
            summed = summed + mul(activated, outer_in[at, :])
        normal_two, root_two = normalize(summed)
        output_ref[...] = mask * (normal_two * line(3) + line(4))
        err_two = mask * cot_ref[...]
        rest_two = back_normalize(err_two * line(3), normal_two, root_two)
        rest_two_ref[...] = rest_two
        sums_ref[0:1, :] += total(rest_two)
        sums_ref[3:4, :] += total(err_two * normal_two)
        sums_ref[4:5, :] += total(err_two)
        err_one = rest_two
        for tile in range(tiles):
            at = slice(tile * width, (tile + 1) * width)
            dinner = mul(rest_two, outer_in[at, :], NT) * slope_ref[:, at]
            dinner_ref[:, at] = dinner
            bias_sums_ref[0:1, at] += total(dinner)
            err_one = err_one + mul(dinner, inner_in[:, at], NT)
        normal_one, root_one = normal_ref[...], root_ref[:, 0:1]
        rest_one = back_normalize(err_one * line(1), normal_one, root_one)
        rest_one_ref[...] = rest_one
        sums_ref[1:2, :] += total(err_one * normal_one)
        sums_ref[2:3, :] += total(err_one)
        dattended_ref[...] = mul(rest_one, mixer_in[...], NT)


def back_state_kernel(
    info_ref, da_ref, attended_ref, den_ref, query_ref, trig_ref, dtot_ref, dden_ref, out_ref, scratch
):
    valid = chunk_valid(info_ref)

    @pl.when(jnp.logical_not(valid))
    def _():
        zero(dtot_ref, dden_ref, out_ref)

    @pl.when(valid)
    def _():
        rows, width = query_ref.shape
        cos, sin = angles(trig_ref, rows)
        first = first_head((rows, LANES))
        lane = lane_of((rows, LANES))
        ddens = jnp.zeros((rows, LANES), jnp.float32)
        for pair in range(width // LANES):
            at = slice(pair * LANES, (pair + 1) * LANES)
            grad = da_ref[:, at]
            both = grad * attended_ref[:, at]
            for head in range(2):
                column = 2 * pair + head
                own = first if head == 0 else ~first
                den = den_ref[:, column : column + 1]
                part = jnp.sum(jnp.where(own, both, 0.0), axis=1, keepdims=True)
                change = jnp.where(den > 1.0, -part / jnp.maximum(den, 1.0), 0.0)
                ddens = jnp.where(lane == column, jnp.broadcast_to(change, (rows, LANES)), ddens)
            one = jnp.broadcast_to(den_ref[:, 2 * pair : 2 * pair + 1], (rows, LANES))
            two = jnp.broadcast_to(den_ref[:, 2 * pair + 1 : 2 * pair + 2], (rows, LANES))
            dtot_ref[:, at] = grad / jnp.maximum(jnp.where(first, one, two), 1.0)
        dden_ref[...] = ddens
        ones = []
        for pair in range(width // LANES):
            query = query_ref[:, pair * LANES : (pair + 1) * LANES]
            feature = jnp.concatenate([query * cos, query * sin], axis=1)
            ones.append(pair_state(dtot_ref, ddens, pair, feature, scratch))
        store_state(scratch, ones, out_ref)


def back_near_kernel(
    info_ref, query_ref, key_ref, value_ref, dtot_ref, dden_ref, trig_ref, gate_ref, state_ref, other_ref,
    dquery_ref, dkey_ref, dvalue_ref, scratch,
):
    valid = chunk_valid(info_ref)

    @pl.when(jnp.logical_not(valid))
    def _():
        zero(dquery_ref, dkey_ref, dvalue_ref)

    @pl.when(valid)
    def _():
        rows, width = query_ref.shape
        pairs = width // LANES
        cos, sin = angles(trig_ref, rows)
        gate = gate_ref[0]
        load_state(info_ref, state_ref, other_ref, scratch)
        first = first_head((rows, LANES))
        lane = lane_of((rows, LANES))
        for pair in range(pairs):
            at = slice(pair * LANES, (pair + 1) * LANES)
            query, key, value, dtot = query_ref[:, at], key_ref[:, at], value_ref[:, at], dtot_ref[:, at]
            drops = [dden_ref[:, 2 * pair + head : 2 * pair + head + 1] for head in range(2)]
            weight = jnp.where(
                lane == 0,
                jnp.broadcast_to(drops[0], (rows, LANES)),
                jnp.where(lane == 1, jnp.broadcast_to(drops[1], (rows, LANES)), 0.0),
            )
            before = mul(jnp.concatenate([dtot, weight], axis=1), pair_matrix(scratch, pair, pairs))
            dquery = before[:, :LANES] * cos + before[:, LANES:] * sin
            dkey = jnp.zeros((rows, LANES), jnp.float32)
            dvalue = jnp.zeros((rows, LANES), jnp.float32)
            for head in range(2):
                own = first if head == 0 else ~first
                query_own = jnp.where(own, query, 0.0)
                dtot_own = jnp.where(own, dtot, 0.0)
                scores = mul(query_own, key, NT) * gate
                back = (mul(dtot_own, value, NT) + drops[head]) * gate
                dquery = dquery + mul(back, jnp.where(own, key, 0.0))
                dkey = dkey + mul(back, query_own, TN)
                dvalue = dvalue + mul(scores, dtot_own, TN)
            dquery_ref[:, at] = jnp.where(query > 0.0, dquery, 0.0)
            dkey_ref[:, at] = dkey
            dvalue_ref[:, at] = dvalue


def back_far_kernel(
    info_ref, key_ref, value_ref, dquery_in, dkey_in, dvalue_in, trig_ref, grad_ref, other_ref, out_ref, scratch
):
    valid = chunk_valid(info_ref)

    @pl.when(jnp.logical_not(valid))
    def _():
        zero(out_ref)

    @pl.when(valid)
    def _():
        rows, width = key_ref.shape
        pairs = width // LANES
        cos, sin = angles(trig_ref, rows)
        load_state(info_ref, grad_ref, other_ref, scratch)
        lane = lane_of((rows, LANES))
        for pair in range(pairs):
            at = slice(pair * LANES, (pair + 1) * LANES)
            key, value = key_ref[:, at], value_ref[:, at]
            after = pair_matrix(scratch, pair, pairs)
            counted = jnp.concatenate([value, jnp.where(lane < 2, 1.0, 0.0)], axis=1)
            onward = mul(counted, after)
            feature = jnp.concatenate([key * cos, key * sin], axis=1)
            dvalue = dvalue_in[:, at] + mul(feature, after, NT)[:, :LANES]
            dkey = dkey_in[:, at] + onward[:, :LANES] * cos + onward[:, LANES:] * sin
            side, place = divmod(pair, pairs // 2)
            grads = (dquery_in[:, at], jnp.where(key > 0.0, dkey, 0.0), dvalue)
            for number, grad in enumerate(grads):
                start = number * (width // 2) + place * LANES
                out_ref[side, :, start : start + LANES] = grad


def tokens_kernel(
    info_ref, rest_ref, grads_ref, query_own, query_1, query_2, query_3, query_4,
    key_own, value_own, pack_1, pack_2, pack_3, pack_4, out_ref, query_in, key_in, value_in, sems,
):
    groups = [
        (query_own, (query_1, query_2, query_3, query_4), 0, 1, query_in),
        (key_own, (pack_1, pack_2, pack_3, pack_4), 0, 1, key_in),
        (value_own, (pack_1, pack_2, pack_3, pack_4), key_own.shape[1], 1, value_in),
    ]
    load_once(info_ref, groups, sems)
    valid = chunk_valid(info_ref)

    @pl.when(jnp.logical_not(valid))
    def _():
        zero(out_ref)

    @pl.when(valid)
    def _():
        half = out_ref.shape[1] // 2
        total = rest_ref[...]
        for number, weight in enumerate((query_in, key_in, value_in)):
            at = slice(number * half, (number + 1) * half)
            grad = jnp.concatenate([grads_ref[0, :, at], grads_ref[1, :, at]], axis=1)
            total = total + mul(grad, weight[...], NT)
        out_ref[...] = total


def scan_kernel(order_ref, states_ref, out_ref):
    chips = states_ref.shape[0]
    first, cut = order_ref[0], order_ref[1] > 0
    chip = lambda number: lax.rem(first + number, chips)
    zeros = jnp.zeros(states_ref.shape[2:], jnp.float32)

    def early(number, carry):
        running, others = carry
        at = chip(number)
        out_ref[at, 0] = running
        return running + states_ref[at, 0], others + states_ref[at, 0]

    running, others = lax.fori_loop(1, chips, early, (states_ref[first, 0], zeros))
    out_ref[first, 0] = jnp.where(cut, others, zeros)
    running = jnp.where(cut, running + states_ref[first, 1], running)

    def late(number, carry):
        running, others = carry
        at = chip(chips - number)
        out_ref[at, 1] = running
        return running + states_ref[at, 1], others + states_ref[at, 1]

    running, others = lax.fori_loop(1, chips, late, (running, others))
    out_ref[first, 1] = jnp.where(cut, others, running)


def scan_states(place, states, rotation, reverse, between):
    chips = place.size // 2
    chip = place.index // 2
    one, two = (1, 0) if reverse else (0, 1)
    own = states[0]
    got = place.swap(states[1], 0)
    wrap = place.size - lax.dynamic_index_in_dim(rotation, place.core, 0, False)
    cut = wrap == 2 * chip + 1
    lower, upper = jnp.where(place.core == 0, own, got), jnp.where(place.core == 0, got, own)
    combined = jnp.stack(
        [
            jnp.where(cut, upper[:, one], lower[:, one] + upper[:, one]),
            jnp.where(cut, lower[:, two] + lower[:, one], lower[:, two] + upper[:, two]),
        ],
        axis=1,
    )
    groups = [[2 * number + core for number in range(chips)] for core in range(2)]
    exchange = lambda array: lax.all_to_all(array, "ctx", 0, 0, axis_index_groups=groups, tiled=True)
    gathered = exchange(combined)
    extra = between(combined, 0)
    gathered = after(gathered, *extra)
    order = jnp.stack([(wrap // 2) % chips, wrap % 2]).astype(jnp.int32)
    whole = pl.BlockSpec(gathered.shape, lambda i, s: (0, 0, 0, 0))
    summed = pl.pallas_call(
        scan_kernel,
        grid_spec=pltpu.PrefetchScalarGridSpec(
            num_scalar_prefetch=1, grid=(1,), in_specs=[whole], out_specs=whole
        ),
        out_shape=jax.ShapeDtypeStruct(gathered.shape, jnp.float32),
        compiler_params=params(),
        cost_estimate=cost(gathered.size, 8 * gathered.size),
        name="scan_states",
    )(order, gathered)
    base = exchange(summed)
    base = after(base, *between(summed, 1))
    both = lower[:, one] + upper[:, one]
    low = [
        jnp.where(cut, base[:, 0] + upper[:, one], base[:, 0]),
        jnp.where(cut, base[:, 0] + both, base[:, 1] + upper[:, two]),
    ]
    high = [
        jnp.where(cut, 0.0, base[:, 0] + lower[:, one]),
        jnp.where(cut, base[:, 1] + both + lower[:, two], base[:, 1]),
    ]
    stay = jnp.stack([jnp.where(place.core == 0, low[half], high[half]) for half in (one, two)], axis=1)
    leave = jnp.stack([jnp.where(place.core == 0, high[half], low[half]) for half in (one, two)], axis=1)
    return stay, place.swap(leave, 0)


def per_device(
    tokens, w_query, w_key, w_value, w_mixer, w_inner, b_inner, w_outer, b_outer,
    gain_one, shift_one, gain_two, shift_two, seq_lengths, rotation, cotangent,
):
    place = Place()
    slots, slot_rows, width = tokens.shape
    rows = slots * slot_rows
    half_rows = slot_rows // 2
    chunks = slots * 2
    heads = HEADS
    pairs = heads // 2
    parts = place.size // 2
    state_rows = pairs * (LANES // 2) + pairs
    step = -(-state_rows // parts)
    step = -(-step // 8) * 8
    state_shape = (slots, parts, 2, step, 2 * LANES)

    first_slot = place.pair * slots
    lengths = lax.dynamic_slice_in_dim(seq_lengths, first_slot, slots)
    turns = lax.dynamic_slice_in_dim(rotation, first_slot, slots)
    group = (place.index + turns) % place.size
    within = jnp.arange(slot_rows, dtype=jnp.int32)
    per_group = half_rows // SPAN
    block = within // SPAN
    spans = place.size * 2 * per_group
    early = group[:, None] * per_group + block[None, :]
    late = spans - 1 - (group[:, None] * per_group + block[None, :] - per_group)
    spot = jnp.where(block[None, :] < per_group, early, late) * SPAN + (within % SPAN)[None, :]
    valid = (spot < lengths[:, None]).astype(jnp.float32)
    angle = 0.5 * math.pi * spot.astype(jnp.float32) / lengths[:, None].astype(jnp.float32)
    cos, sin = jnp.cos(angle) * valid, jnp.sin(angle) * valid
    trig = jnp.pad(
        jnp.stack([cos, sin, valid], axis=-1).reshape(rows, 3), ((0, 0), (0, LANES - 3))
    )
    cut = lambda array: array.reshape(chunks, half_rows)
    pos, cos_cut, sin_cut = cut(spot), cut(cos), cut(sin)
    gate = jnp.where(
        pos[:, None, :] <= pos[:, :, None],
        cos_cut[:, :, None] * cos_cut[:, None, :] + sin_cut[:, :, None] * sin_cut[:, None, :],
        0.0,
    )
    info = jnp.concatenate(
        [
            jnp.stack([place.pair, place.core, place.bit(1), place.bit(2)]).astype(jnp.int32),
            jnp.max(valid.reshape(chunks, half_rows), axis=1).astype(jnp.int32),
        ]
    )

    vectors = jnp.concatenate([b_inner, b_outer, gain_one, shift_one, gain_two, shift_two])
    pack_1 = fetch(place, jnp.concatenate([w_key, w_value], axis=1), 1)
    narrow_1 = fetch(place, jnp.concatenate([w_query, w_mixer], axis=1), 1, pack_1)
    other_vectors = place.swap(after(vectors, pack_1), "fsdp")
    inner_1 = fetch(place, w_inner, 1, pack_1)
    outer_1 = fetch(place, w_outer, 2, pack_1)
    pack_2 = place.swap(pack_1, 1)
    pack_w = (pack_1, pack_2, place.swap(pack_1, 0), place.swap(pack_2, 0))
    sizes = [b_inner.shape[0]] + [width // 2] * 5
    whole, offset = [], 0
    for size in sizes:
        whole.append(
            in_order(place.pair, vectors[offset : offset + size], other_vectors[offset : offset + size])
        )
        offset += size
    bias = jnp.pad(whole[0].reshape(1, -1), ((0, 7), (0, 0)))
    lines = jnp.pad(jnp.stack(whole[1:]), ((0, 3), (0, 0)))

    flat = tokens.reshape(rows, width)
    wide = w_inner.shape[1]
    row_spec = pl.BlockSpec((half_rows, width), lambda i, s: (i, 0))
    wide_spec = pl.BlockSpec((half_rows, wide), lambda i, s: (i, 0))
    lane_spec = pl.BlockSpec((half_rows, LANES), lambda i, s: (i, 0))
    gate_spec = pl.BlockSpec((1, half_rows, half_rows), lambda i, s: (i, 0, 0))
    state_spec = pl.BlockSpec(
        (1, parts, 1, step, 2 * LANES), lambda i, s: (lax.div(i, 2) ^ s[1], 0, lax.rem(i, 2), 0, 0)
    )
    sum_specs = [pl.BlockSpec((parts, 1, step, 2 * LANES), lambda i, s: (0, lax.rem(i, 2), 0, 0))] * 2
    fixed = lambda array: pl.BlockSpec(array.shape, lambda i, s: (0,) * len(array.shape))
    piece_spec = pl.BlockSpec(memory_space=pl.ANY)
    shaped = lambda *shape: jax.ShapeDtypeStruct(shape, jnp.float32)
    row_type, wide_type, lane_type = shaped(rows, width), shaped(rows, wide), shaped(rows, LANES)
    state_type = shaped(*state_shape)
    state_scratch = pltpu.VMEM((parts * step, 2 * LANES), jnp.float32)
    square = pltpu.VMEM((width, width), jnp.float32)
    copies = lambda count: pltpu.SemaphoreType.DMA((count, 5))

    def call(kernel, name, in_specs, out_specs, out_shape, scratch, work, *operands):
        return pl.pallas_call(
            kernel,
            grid_spec=pltpu.PrefetchScalarGridSpec(
                num_scalar_prefetch=1,
                grid=(chunks,),
                in_specs=in_specs,
                out_specs=out_specs,
                scratch_shapes=scratch,
            ),
            out_shape=out_shape,
            compiler_params=params(),
            cost_estimate=cost(*work),
            name=name,
        )(info, *operands)

    key, value, states = call(
        key_kernel, "key_states", [row_spec, lane_spec] + [piece_spec] * 6,
        [row_spec, row_spec, state_spec], [row_type, row_type, state_type],
        [square, square, state_scratch, copies(2)], (1e10, 16e6),
        flat, trig, w_key, w_value, *pack_w,
    )
    narrow_2 = place.swap(narrow_1, 1)
    narrow_3, narrow_4 = place.swap(narrow_1, 0), place.swap(narrow_2, 0)
    narrow_w = (narrow_1, narrow_2, narrow_3, narrow_4)
    forward = {}

    def while_forward(sent, number):
        if number == 0:
            return (narrow_2,)
        forward["query"] = call(
            query_kernel, "query", [row_spec] + [piece_spec] * 5, row_spec, row_type,
            [square, copies(1)], (6e9, 8e6), after(flat, sent), w_query, *narrow_w,
        )
        return (forward["query"],)

    inner_2 = place.swap(inner_1, 1)
    outer_2 = place.swap(outer_1, 2)
    before = scan_states(place, after(states, narrow_2, inner_1), turns, False, while_forward)
    query = forward["query"]
    inner_w = (w_inner, inner_1, inner_2, place.swap(inner_1, 0), place.swap(after(inner_2, before[0]), 0))
    outer_w = (w_outer, outer_1, outer_2, place.swap(outer_1, 0), place.swap(after(outer_2, before[0]), 0))
    attended, den = call(
        attend_kernel, "attend", [row_spec] * 3 + [lane_spec, gate_spec] + sum_specs,
        [row_spec, lane_spec], [row_type, lane_type], [state_scratch], (1e10, 12e6),
        query, key, value, trig, gate, *before,
    )
    sums_type, bias_sums_type = shaped(8, width), shaped(8, wide)
    output, hidden, activated, rest_two, dinner, rest_one, dattended, sums, bias_sums = call(
        layer_kernel, "layer",
        [row_spec] * 3 + [lane_spec, fixed(lines), fixed(bias)] + [piece_spec] * 15,
        [row_spec, row_spec, wide_spec, row_spec, wide_spec, row_spec, row_spec, fixed(sums_type), fixed(bias_sums_type)],
        [row_type, row_type, wide_type, row_type, wide_type, row_type, row_type, sums_type, bias_sums_type],
        [
            square,
            pltpu.VMEM((width, wide), jnp.float32),
            pltpu.VMEM((wide, width), jnp.float32),
            pltpu.VMEM((half_rows, wide), jnp.float32),
            pltpu.VMEM((half_rows, width), jnp.float32),
            pltpu.VMEM((half_rows, LANES), jnp.float32),
            copies(3),
        ],
        (5e10, 70e6),
        flat, attended, cotangent.reshape(rows, width), trig, lines, bias,
        w_mixer, *narrow_w, *inner_w, *outer_w,
    )
    def part(array, number, count):
        size = array.shape[1] // count
        return lax.dynamic_slice_in_dim(array, number * size, size, 1)

    def by_columns(left, right, core):
        return mul(left, part(right, core, 2), TN).reshape(2, left.shape[1] // 2, -1)

    def by_rows(left, right, core):
        return jnp.stack([mul(part(left, 2 * side + core, 4), right, TN) for side in range(2)])

    here, there = place.core, 1 - place.core

    small = jnp.concatenate(
        [bias_sums[0].reshape(2, -1)] + [sums[line].reshape(2, -1) for line in range(5)], axis=1
    )
    small = small.reshape(2, width // 2, -1)
    small_width = small.shape[2]
    small = jnp.pad(small, ((0, 0), (0, 0), (0, LANES - small_width)))
    outer_leave = by_rows(activated, rest_two, there)
    outer_got = place.swap(outer_leave, 0)
    dtot, dden, back_states = call(
        back_state_kernel, "query_states", [row_spec, row_spec, lane_spec, row_spec, lane_spec],
        [row_spec, lane_spec, state_spec], [row_type, lane_type, state_type], [state_scratch], (4e9, 12e6),
        after(dattended, outer_leave), attended, den, query, trig,
    )
    outer_sum = Reduction(place, [[by_rows(activated, after(rest_two, back_states), here) + outer_got]])
    first_sent = outer_sum.advance()
    backward = {}

    def while_backward(sent, number):
        if number == 0:
            inner_leave = by_columns(hidden, after(dinner, sent, *first_sent), there)
            mixer_leave = by_columns(attended, after(rest_one, inner_leave), there)
            small_total = small + place.swap(after(small, inner_leave), 0)
            inner_got, mixer_got = place.swap(inner_leave, 0), place.swap(mixer_leave, 0)
            inner_grad = by_columns(hidden, after(dinner, mixer_leave), here) + inner_got
            mixer_grad = by_columns(attended, after(rest_one, inner_grad), here) + mixer_got
            backward["inner"] = Reduction(place, [[inner_grad], [mixer_grad], [small_total]])
            return (mixer_grad,)
        moved = advance_all([outer_sum, backward["inner"]], [sent])
        backward["near"] = call(
            back_near_kernel, "back_near",
            [row_spec] * 4 + [lane_spec, lane_spec, gate_spec] + sum_specs, [row_spec] * 3, [row_type] * 3,
            [state_scratch], (2e10, 24e6),
            query, key, value, after(dtot, *moved), dden, trig, gate, *before,
        )
        return advance_all([backward["inner"], outer_sum], [backward["near"][0]])

    behind = scan_states(place, back_states, turns, True, while_backward)
    inner_sum = backward["inner"]
    half = width // 2
    grads_spec = pl.BlockSpec((2, half_rows, 3 * half), lambda i, s: (0, i, 0))
    grads = call(
        back_far_kernel, "back_far", [row_spec] * 5 + [lane_spec] + sum_specs, grads_spec,
        shaped(2, rows, 3 * half), [state_scratch], (4e9, 16e6),
        key, value, *backward["near"], trig, *behind,
    )
    moved = advance_all([outer_sum, inner_sum], [grads])
    side_gradient = lambda values, core: mul(
        flat, lax.dynamic_index_in_dim(values, core, 0, False), TN
    ).reshape(2, half, 3 * half)
    leave = side_gradient(after(grads, *moved), there)
    got = place.swap(leave, 0)
    grad_tokens = call(
        tokens_kernel, "grad_tokens", [row_spec, grads_spec] + [piece_spec] * 11, row_spec, row_type,
        [square] * 3 + [copies(3)], (1e10, 18e6),
        after(rest_one, leave), grads, w_query, *narrow_w, w_key, w_value, *pack_w,
    )
    core = place.core.reshape(1).astype(jnp.int32)
    moved = advance_all([outer_sum, inner_sum], [grad_tokens])
    attention_sum = Reduction(place, [[side_gradient(after(grads, *moved), here) + got]])
    moved = []
    waves = len(attention_sum.orders[0]) + len(attention_sum.back[0]) + 1
    for wave in range(waves):
        active = [attention_sum]
        if wave < waves - 4:
            active.append(inner_sum)
        if wave < waves - 5:
            active.append(outer_sum)
        moved = advance_all(active, moved)
        if wave == waves - 5:
            outer_mine, outer_other = outer_sum.result
            grad_outer = join(core, outer_mine, outer_other, 0, 1, width, 0)
            moved.append(grad_outer)
        if wave == waves - 3:
            inner_mine, inner_other = inner_sum.result
            grad_inner = join(core, inner_mine, inner_other, 0, 1, wide // 2, 1)
            grad_mixer = join(core, inner_mine, inner_other, wide // 2, 1, half, 1)
            moved += [grad_inner, grad_mixer]
    third_mine, third_other = attention_sum.result
    narrow = lax.slice_in_dim(inner_mine, wide // 2 + half, wide // 2 + half + small_width, axis=1).reshape(-1)
    vector_grads, offset = [], 0
    for size in sizes:
        vector_grads.append(narrow[offset : offset + size])
        offset += size
    grad_inbias, grad_outbias, grad_gain_one, grad_shift_one, grad_gain_two, grad_shift_two = vector_grads
    grad_query, grad_key, grad_value = [
        join(core, third_mine, third_other, number * half, 1, half, 1) for number in range(3)
    ]
    return (
        output.reshape(tokens.shape),
        grad_tokens.reshape(tokens.shape),
        grad_query,
        grad_key,
        grad_value,
        grad_mixer,
        grad_inner,
        grad_inbias,
        grad_outer,
        grad_outbias,
        grad_gain_one,
        grad_shift_one,
        grad_gain_two,
        grad_shift_two,
    )


def solution(mesh):
    rows = P("fsdp", "ctx", None)
    matrix = P("fsdp", None)
    vector = P("fsdp")
    in_specs = (
        rows, matrix, matrix, matrix, matrix, matrix, vector, matrix, vector,
        vector, vector, vector, vector, P(), P(), rows,
    )
    out_specs = (
        rows, rows, matrix, matrix, matrix, matrix, matrix, vector, matrix,
        vector, vector, vector, vector, vector,
    )
    return jax.shard_map(
        per_device, mesh=mesh, in_specs=in_specs, out_specs=out_specs, check_vma=False
    )
```
